256 devices in a mesh: dp: 128 (over y_hi, x, z, core), pipe: 2 (over y_lo).
Axes of the slice: x: 4, y: 4 (y_hi: 2, y_lo: 2; y = y_hi * 2 + y_lo), z: 8, core: 2. Of those that a mesh axis runs over, the one named last changes fastest.
Arguments:
- block_input: bfloat16 [2, 32768, 1536], P('pipe', 'dp'), may hold values from -100 to 100
- saved_qkv: bfloat16 [2, 32768, 4608], P('pipe', 'dp'), may hold values from -10 to 10
- cotangent: bfloat16 [2, 32768, 1536], P('pipe', 'dp'), may hold values from -6 to 6
- mod_table: float32 [2, 3, 1536], P('pipe'), may hold values from -3 to 3
- clip_condition: float32 [2, 1024, 4608], P('pipe', 'dp'), may hold values from -3 to 3
- clip_frames: int32 [2, 1024], P('pipe', 'dp'), may hold values from 0 to 8, as said below
- frame_tokens: int32 [2, 1024], P('pipe', 'dp'), may hold values from 2 to 64, as said below
- tile_layout: int32 [2, 256, 2], P('pipe', 'dp'), may hold values from 0 to 1, as said below
- frozen_qkv: bfloat16 [2, 1536, 4608], P('pipe', 'dp'), may hold values from -0.15625 to 0.15625
- frozen_out: bfloat16 [2, 1536, 1536], P('pipe', 'dp'), may hold values from -0.15625 to 0.15625
- adapters: bfloat16 [2, 9216, 128], P('pipe'), may hold values from -0.15625 to 0.15625
Outputs:
- upstream: bfloat16 [2, 32768, 1536], P('pipe', 'dp')
- d_table: float32 [2, 3, 1536], P('pipe')
- d_adapters: float32 [2, 9216, 128], P('pipe', 'dp')
The draws below stay inside these ranges and needn't reach their ends.
Inputs may be any that keep to these rules, and one draw needn't show every extreme that they name: `clip_frames`: clips are packed in slot order; a slot with 0 frames holds no clip and so does every later slot of that device; the clips of one device hold at most 256 tokens. `frame_tokens`: even. `tile_layout`: every diagonal tile is live.
All inputs are finite; a program needn't handle non-finite values.
Results may differ from the reference program's by a relative error of at most 0.0065.
Values may be sent and summed in bfloat16 or wider, within the bound.
A program may use at most 128 MiB of HBM per device.

```python
import math
import jax
import jax.numpy as jnp
from jax import lax

D = 1536
HEADS = 12
HEAD = 128
RANK = 128
TOK_DEV = 256
TILE = 128
CLIPS = 8
FRAME_MAX = 8
PER_FRAME_MAX = 64
SECTIONS = 2
TOKENS = 32768
HD = 1536
TILES = 2
TILE_ROWS = 256
CLIP_SLOTS = 1024
ADAPT_ROWS = 9216
N_DP = 128


def clip_plan(key):
    frame_key = jax.random.fold_in(key, 31)
    size_key = jax.random.fold_in(key, 37)
    grid = (SECTIONS, CLIP_SLOTS // CLIPS, CLIPS)
    counts = jax.random.randint(frame_key, grid, 1, FRAME_MAX + 1)
    widths = 2 * jax.random.randint(size_key, grid, 1, PER_FRAME_MAX // 2 + 1)
    clip_ends = jnp.cumsum(counts * widths, axis=2)
    kept = jnp.where(clip_ends <= TOK_DEV, counts, 0)
    return (kept.reshape(SECTIONS, CLIP_SLOTS).astype(jnp.int32), widths.reshape(SECTIONS, CLIP_SLOTS).astype(jnp.int32))


def draw_clip_frames(key, part):
    return clip_plan(key)[0]


def draw_frame_tokens(key, part):
    return clip_plan(key)[1]


def draw_tile_layout(key, part):
    grid = (SECTIONS, TILE_ROWS // TILES, TILES, TILES)
    random_live = jax.random.randint(key, grid, 0, 2)
    diagonal = (jnp.arange(TILES)[:, None] == jnp.arange(TILES)[None, :]).astype(jnp.int32)
    return jnp.maximum(random_live, diagonal[None, None]).reshape(SECTIONS, TILE_ROWS, TILES).astype(jnp.int32)


def draw_block_input(key, part):
    shape = (SECTIONS, TOKENS, D)
    row_scale = jnp.exp(jax.random.uniform(jax.random.fold_in(key, 3), (SECTIONS, TOKENS, 1), jnp.float32, math.log(0.5), math.log(5.0)))
    column_scale = jnp.exp(jax.random.uniform(jax.random.fold_in(key, 4), (SECTIONS, 1, D), jnp.float32, math.log(0.5), math.log(5.0)))
    base = jnp.clip(jax.random.normal(jax.random.fold_in(key, 7), shape, jnp.float32), -4.0, 4.0)
    return (base * row_scale * column_scale).astype(jnp.bfloat16)


def draw_saved_qkv(key, part):
    shape = (SECTIONS, TOKENS, 3, HEADS, HEAD)
    result = jnp.clip(jax.random.normal(jax.random.fold_in(key, 8), shape, jnp.float32), -4.0, 4.0)
    return result.reshape(SECTIONS, TOKENS, 3 * HEADS * HEAD).astype(jnp.bfloat16)


def shard_levels(rng, extent, shards, smallest, largest):
    def one(dim, blocks):
        heights = jax.random.uniform(jax.random.fold_in(jax.random.fold_in(rng, 6), dim), (blocks,), jnp.float32, smallest / len(shards), largest / len(shards))
        return jnp.repeat(jnp.exp(heights), extent[dim] // blocks).reshape((-1,) + (1,) * (len(extent) - dim - 1))

    loudness = one(*shards[0])
    for cut in shards[1:]:
        loudness = loudness * one(*cut)
    return loudness


def noise(key, shape, deviation, most, shards=(), held_as=jnp.bfloat16):
    factor_of = shard_levels(key, shape, shards, -0.22, 0.18) if shards else 1.0
    values = jax.random.normal(key, shape, jnp.float32) * deviation * factor_of
    return jnp.minimum(jnp.maximum(values, -most), most).astype(held_as)


def setup_inputs(seed: int = 0) -> dict:
    streams_of = jax.random.split(jax.random.key(seed), 12)
    block_input = draw_block_input(jax.random.fold_in(streams_of[11], 71), 0)
    saved_qkv = draw_saved_qkv(jax.random.fold_in(streams_of[11], 71), 0)
    cotangent = noise(streams_of[2], (SECTIONS, TOKENS, D), 1.0, 6.0, ((0, 2), (1, 128)))
    mod_table = noise(streams_of[3], (SECTIONS, 3, D), 0.5, 3.0, ((0, 2),), jnp.float32)
    clip_condition = noise(streams_of[4], (SECTIONS, CLIP_SLOTS, 3 * D), 0.5, 3.0, ((0, 2), (1, 128)), jnp.float32)
    clip_frames = draw_clip_frames(jax.random.fold_in(streams_of[11], 71), 0)
    frame_tokens = draw_frame_tokens(jax.random.fold_in(streams_of[11], 71), 0)
    tile_layout = draw_tile_layout(jax.random.fold_in(streams_of[11], 71), 0)
    frozen_qkv = noise(streams_of[8], (SECTIONS, D, 3 * HD), D ** -0.5, 0.15625, ((0, 2), (1, 128)))
    frozen_out = noise(streams_of[9], (SECTIONS, HD, D), HD ** -0.5, 0.15625, ((0, 2), (1, 128)))
    adapters = noise(streams_of[10], (SECTIONS, ADAPT_ROWS, RANK), D ** -0.5, 0.15625, ((0, 2),))
    return dict(block_input=block_input, saved_qkv=saved_qkv, cotangent=cotangent, mod_table=mod_table, clip_condition=clip_condition, clip_frames=clip_frames, frame_tokens=frame_tokens, tile_layout=tile_layout, frozen_qkv=frozen_qkv, frozen_out=frozen_out, adapters=adapters)


EPSILON = 1e-06
HIGH = lax.Precision.HIGHEST

def clip_index(frame_counts, frame_sizes, rows):
    clip_ends = jnp.cumsum(frame_counts * frame_sizes).astype(jnp.int32)
    position = jnp.arange(rows, dtype=jnp.int32)
    return lax.optimization_barrier(jnp.sum((position[:, None] >= clip_ends[None, :]).astype(jnp.int32), axis=1))

def device_terms(tokens_here, saved, cotangent_here, condition, frame_counts, frame_sizes, layout, table, frozen_in, frozen_back, adapter_rows):
    rows = tokens_here.shape[0]
    down_qkv = adapter_rows[:D]
    up_qkv = adapter_rows[D:D + 3 * HD]
    down_out = adapter_rows[D + 3 * HD:D + 4 * HD]
    up_out = adapter_rows[D + 4 * HD:]
    clip_of = clip_index(frame_counts, frame_sizes, rows)
    onehot_clip = (clip_of[:, None] == jnp.arange(CLIPS, dtype=jnp.int32)[None, :]).astype(jnp.float32)
    modulation = table.reshape(1, 3 * D) + jnp.dot(onehot_clip, condition, precision=HIGH)
    shift_rows = modulation[:, :D]
    scale_rows = modulation[:, D:2 * D]
    gate_rows = modulation[:, 2 * D:]
    inputs_f = tokens_here.astype(jnp.float32)
    centered = inputs_f - lax.optimization_barrier(jnp.mean(inputs_f, axis=1, keepdims=True))
    inverse = lax.rsqrt(lax.optimization_barrier(jnp.mean(centered * centered, axis=1, keepdims=True)) + EPSILON)
    normed = centered * inverse
    modded = (normed * (1.0 + scale_rows) + shift_rows).astype(jnp.bfloat16)
    position = jnp.arange(rows, dtype=jnp.int32)
    tile_of = position // TILE
    live_pairs = layout[tile_of][:, tile_of] > 0
    allowed = live_pairs & (clip_of[:, None] == clip_of[None, :])
    queries = saved[:, :HD].reshape(rows, HEADS, HEAD).astype(jnp.float32)
    key_rows = saved[:, HD:2 * HD].reshape(rows, HEADS, HEAD).astype(jnp.float32)
    value_rows = saved[:, 2 * HD:].reshape(rows, HEADS, HEAD).astype(jnp.float32)
    factor = HEAD ** (-0.5)
    scores = jnp.einsum('qhd,khd->hqk', queries, key_rows) * factor
    scores = jnp.where(allowed[None], scores, -jnp.inf)
    probs = jax.nn.softmax(scores, axis=2)
    probs_b = probs.astype(jnp.bfloat16).astype(jnp.float32)
    attention = jnp.einsum('hqk,khd->qhd', probs_b, value_rows).reshape(rows, HD).astype(jnp.bfloat16)
    low_out = jnp.dot(attention, down_out, preferred_element_type=jnp.float32).astype(jnp.bfloat16)
    branch = jnp.dot(attention, frozen_back, preferred_element_type=jnp.float32) + jnp.dot(low_out, up_out.T, preferred_element_type=jnp.float32)
    cotangent_f = cotangent_here.astype(jnp.float32)
    gated = (gate_rows * cotangent_f).astype(jnp.bfloat16)
    low_grad_out = jnp.dot(gated, up_out, preferred_element_type=jnp.float32).astype(jnp.bfloat16)
    grad_attention = (jnp.dot(gated, frozen_back.T, preferred_element_type=jnp.float32) + jnp.dot(low_grad_out, down_out.T, preferred_element_type=jnp.float32)).astype(jnp.bfloat16)
    grad_heads = grad_attention.reshape(rows, HEADS, HEAD).astype(jnp.float32)
    grad_probs = jnp.einsum('qhd,khd->hqk', grad_heads, value_rows)
    delta = lax.optimization_barrier(jnp.sum(probs * grad_probs, axis=2, keepdims=True))
    grad_scores = (probs * (grad_probs - delta) * factor).astype(jnp.bfloat16).astype(jnp.float32)
    grad_query = jnp.einsum('hqk,khd->qhd', grad_scores, key_rows).reshape(rows, HD)
    grad_key = jnp.einsum('hqk,qhd->khd', grad_scores, queries).reshape(rows, HD)
    grad_value = jnp.einsum('hqk,qhd->khd', probs_b, grad_heads).reshape(rows, HD)
    grad_qkv = jnp.concatenate([grad_query, grad_key, grad_value], axis=1).astype(jnp.bfloat16)
    low_in = jnp.dot(modded, down_qkv, preferred_element_type=jnp.float32).astype(jnp.bfloat16)
    low_grad_in = jnp.dot(grad_qkv, up_qkv, preferred_element_type=jnp.float32).astype(jnp.bfloat16)
    grad_modded = jnp.dot(grad_qkv, frozen_in.T, preferred_element_type=jnp.float32) + jnp.dot(low_grad_in, down_qkv.T, preferred_element_type=jnp.float32)
    grad_normed = grad_modded * (1.0 + scale_rows)
    grad_input = cotangent_f + inverse * (grad_normed - lax.optimization_barrier(jnp.mean(grad_normed, axis=1, keepdims=True)) - normed * lax.optimization_barrier(jnp.mean(grad_normed * normed, axis=1, keepdims=True)))
    table_part = jnp.stack([lax.optimization_barrier(jnp.sum(grad_modded, axis=0)), lax.optimization_barrier(jnp.sum(grad_modded * normed, axis=0)), lax.optimization_barrier(jnp.sum(cotangent_f * branch, axis=0))])
    adapter_part = jnp.concatenate([jnp.dot(modded.T, low_grad_in, preferred_element_type=jnp.float32), jnp.dot(grad_qkv.T, low_in, preferred_element_type=jnp.float32), jnp.dot(attention.T, low_grad_out, preferred_element_type=jnp.float32), jnp.dot(gated.T, low_out, preferred_element_type=jnp.float32)], axis=0)
    return (grad_input.astype(jnp.bfloat16), table_part, adapter_part)

def reference(block_input, saved_qkv, cotangent, mod_table, clip_condition, clip_frames, frame_tokens, tile_layout, frozen_qkv, frozen_out, adapters):
    grads_list = []
    table_list = []
    adapter_list = []
    for section in range(SECTIONS):

        def one_device(carry, pieces):
            table_acc, adapter_acc = carry
            grad_here, table_part, adapter_part = device_terms(pieces[0], pieces[1], pieces[2], pieces[3], pieces[4], pieces[5], pieces[6], mod_table[section], frozen_qkv[section], frozen_out[section], adapters[section])
            return ((table_acc + table_part, adapter_acc + adapter_part), grad_here)
        pieces = (block_input[section].reshape(N_DP, TOK_DEV, D), saved_qkv[section].reshape(N_DP, TOK_DEV, 3 * HD), cotangent[section].reshape(N_DP, TOK_DEV, D), clip_condition[section].reshape(N_DP, CLIPS, 3 * D), clip_frames[section].reshape(N_DP, CLIPS), frame_tokens[section].reshape(N_DP, CLIPS), tile_layout[section].reshape(N_DP, TILES, TILES))
        start_sums = (jnp.zeros((3, D), jnp.float32), jnp.zeros((ADAPT_ROWS, RANK), jnp.float32))
        (table_sum, adapter_sum), grads = lax.scan(one_device, start_sums, pieces)
        grads_list.append(grads.reshape(TOKENS, D))
        table_list.append(table_sum / N_DP)
        adapter_list.append(adapter_sum / N_DP)
    upstream = jnp.roll(jnp.stack(grads_list), -1, axis=0)
    return (upstream, jnp.stack(table_list), jnp.stack(adapter_list))
```

```python
import heapq

import jax
import jax.numpy as jnp
from jax import lax
from jax.experimental import pallas as pl
from jax.experimental.pallas import tpu as pltpu
from jax.sharding import PartitionSpec as P

HEAD = 128
TILE = 128


EPSILON = 1e-06
HIGH = lax.Precision.HIGHEST


def passed_along(block, axis, distance):
    devices = range(lax.axis_size(axis))
    route = [((i - distance) % len(devices), i) for i in devices]
    return lax.ppermute(block, axis, route)


def contract_last(left, right):
    return lax.dot_general(
        left, right, (((1,), (1,)), ((), ())), preferred_element_type=jnp.float32
    )


def contract_first(left, right):
    return lax.dot_general(
        left, right, (((0,), (0,)), ((), ())), preferred_element_type=jnp.float32
    )


MESH = pl.DeviceIdType.MESH
NX, NZ, NY, NC = 4, 8, 2, 2
STEP = {"px": (1, 0), "mx": (3, 0), "pz": (0, 1), "mz": (0, 7)}


def spanning_tree(part):
    edges = {}
    via_plus = (0, 1, 6) if part == 0 else (2, 7)

    def edge(parent, way):
        dx, dz = STEP[way]
        child = ((parent[0] + dx) % NX, (parent[1] + dz) % NZ)
        edges.setdefault(parent, []).append((way, child))

    edge((0, 0), "pz")
    edge((0, 0), "mz")
    edge((0, 1), "pz")
    edge((0, 7), "mz")
    for dz in (0, 1, 2, 6, 7):
        edge((0, dz), "px")
        edge((0, dz), "mx")
        if dz in via_plus:
            edge((1, dz), "px")
        else:
            edge((3, dz), "mx")
    for dx in range(NX):
        edge((dx, 2), "pz")
        edge((dx, 6), "mz")
    for dx in (0, 1):
        edge((dx, 3), "pz")
    for dx in (2, 3):
        edge((dx, 5), "mz")
    return edges


def mirrored(node):
    return ((-node[0]) % NX, (-node[1]) % NZ)


def plan_gather(kinds, lasts, backlog=3.0, latency=1.5, y_time=3.0):
    trees = [spanning_tree(0), spanning_tree(1)]

    def depth_below(part, node):
        return max([1 + depth_below(part, c) for _, c in trees[part].get(node, [])], default=0)

    ready = {way: [] for way in STEP}
    free_at = {way: 0.0 for way in STEP}
    events = []
    program = []
    arrivals = {}
    count = 0

    def push(kind, part, node):
        for way, child in trees[part].get(node, []):
            item = (kind, part, mirrored(node))
            heapq.heappush(
                ready[way],
                (kinds.index(kind), -depth_below(part, node), part, item, child),
            )

    def serve(now):
        for way in STEP:
            while ready[way] and free_at[way] - now < backlog:
                _, _, _, item, child = heapq.heappop(ready[way])
                start = max(now, free_at[way])
                free_at[way] = start + lasts[item[0]]
                program.append((now, "send", way, item))
                got = (item[0], item[1], mirrored(child))
                heapq.heappush(events, (free_at[way] + latency, "recv", way, got, child))

    for kind in kinds:
        push(kind, 0, (0, 0))
        heapq.heappush(events, (y_time + 1.5 * kinds.index(kind), "ywait", "", (kind, 1, (0, 0)), (0, 0)))
    serve(0.0)
    held = {}
    while events:
        now, what, way, item, child = heapq.heappop(events)
        program.append((now, what, way, item))
        push(item[0], item[1], child)
        serve(now)
        row = (item[0], item[1], item[2][1])
        held[row] = held.get(row, 0) + 1
        full = NX - 1 if (item[2][1] == 0 and item[1] == 0) else NX
        if held[row] == full:
            program.append((now, "pair", "", row))
    return program


def place():
    d = lax.axis_index("dp")
    return d // 64, (d // 16) % 4, (d // 2) % 8, d % 2


def at(y, x, z, c):
    return {"dp": ((y * NX + x) * NZ + z) * NC + c}


def greet(others):
    barrier = pltpu.get_barrier_semaphore()
    for other in others:
        pl.semaphore_signal(barrier, inc=1, device_id=other, device_id_type=MESH)
    pl.semaphore_wait(barrier, len(others))


class Gather:
    def __init__(self, program, bufs, send_sem, recv_sem):
        self.program, self.bufs = program, bufs
        self.send_sem, self.recv_sem = send_sem, recv_sem
        self.ids = {}
        self.sent = []
        self.y, self.x, self.z, self.c = place()

    @staticmethod
    def count(program):
        return len(Gather.ids_of(program)[0]) , len(Gather.ids_of(program)[1])

    @staticmethod
    def ids_of(program):
        recv, send = {}, {}
        for _, what, way, item in program:
            if what in ("recv", "ywait", "pair"):
                recv.setdefault((what, item), len(recv))
            if what in ("send", "pair"):
                send.setdefault((what, way, item), len(send))
            if what == "ywait":
                send.setdefault((what, way, item), len(send))
        return recv, send

    def block(self, item):
        kind, part, (dx, dz) = item
        y = self.y if part == 0 else 1 - self.y
        return self.bufs[kind].at[self.c, y, lax.rem(self.x + dx, NX), lax.rem(self.z + dz, NZ)]

    def row(self, item, half):
        kind, part, dz = item
        y = self.y if part == 0 else 1 - self.y
        return self.bufs[kind].at[half, y, :, lax.rem(self.z + dz, NZ)]

    def neighbours(self):
        y, x, z, c = self.y, self.x, self.z, self.c
        return {
            way: at(y, lax.rem(x + dx, NX), lax.rem(z + dz, NZ), c) for way, (dx, dz) in STEP.items()
        } | {"y": at(1 - y, x, z, c), "pair": at(y, x, z, 1 - c)}

    def start(self):
        self.recv_id, self.send_id = self.ids_of(self.program)
        self.near = self.neighbours()
        self.done = []

    def copy(self, src, dst, send, recv, target):
        return pltpu.make_async_remote_copy(
            src_ref=src,
            dst_ref=dst,
            send_sem=self.send_sem.at[send],
            recv_sem=self.recv_sem.at[recv],
            device_id=target,
            device_id_type=MESH,
        )

    def cross(self, kinds):
        for kind in kinds:
            own = self.block((kind, 0, (0, 0)))
            key = ("ywait", (kind, 1, (0, 0)))
            copy = self.copy(own, own, self.send_id[("ywait", "", key[1])], self.recv_id[key], self.near["y"])
            copy.start()
            self.sent.append(copy)

    def step(self, entry):
        _, what, way, item = entry
        if what == "send":
            kind, part, (dx, dz) = item
            sx, sz = STEP[way]
            got = (kind, part, ((dx - sx) % NX, (dz - sz) % NZ))
            ref = self.block(item)
            copy = self.copy(ref, ref, self.send_id[(what, way, item)], self.recv_id[("recv", got)], self.near[way])
            copy.start()
            self.sent.append(copy)
        elif what in ("recv", "ywait"):
            ref = self.block(item)
            self.copy(ref, ref, 0, self.recv_id[(what, item)], self.near["pair"]).wait_recv()
        elif what == "pair":
            ref = self.row(item, self.c)
            copy = self.copy(ref, ref, self.send_id[(what, way, item)], self.recv_id[("pair", item)], self.near["pair"])
            copy.start()
            self.sent.append(copy)

    def pair_wait(self, item):
        ref = self.row(item, 1 - self.c)
        self.copy(ref, ref, 0, self.recv_id[("pair", item)], self.near["pair"]).wait_recv()

    def finish(self):
        for copy in self.sent:
            copy.wait_send()


KINDS = ("o", "q")
PLAN = plan_gather(list(KINDS), {"o": 0.8, "q": 2.4})


def gather_kernel(o_in, q_in, wo, wq, send_sem, recv_sem, local_sem):
    g = Gather(PLAN, {"o": wo, "q": wq}, send_sem, recv_sem)
    g.start()
    greet(list(g.near.values()))
    for i, (kind, ref) in enumerate((("o", o_in), ("q", q_in))):
        pltpu.make_async_copy(ref, g.block((kind, 0, (0, 0))), local_sem.at[i]).start()
    for i, (kind, ref) in enumerate((("o", o_in), ("q", q_in))):
        pltpu.make_async_copy(ref, g.block((kind, 0, (0, 0))), local_sem.at[i]).wait()
    g.cross(KINDS)
    for entry in PLAN:
        g.step(entry)
    for entry in PLAN:
        if entry[1] == "pair":
            g.pair_wait(entry[3])
    g.finish()


def gather_weights(o_in, q_in):
    recv, send = Gather.ids_of(PLAN)
    shapes = [
        jax.ShapeDtypeStruct((NC, NY, NX, NZ) + a.shape, a.dtype) for a in (o_in, q_in)
    ]
    return pl.pallas_call(
        gather_kernel,
        name="gather_weights",
        out_shape=shapes,
        in_specs=[pl.BlockSpec(memory_space=pltpu.VMEM)] * 2,
        out_specs=[pl.BlockSpec(memory_space=pl.ANY)] * 2,
        scratch_shapes=[
            pltpu.SemaphoreType.DMA((len(send),)),
            pltpu.SemaphoreType.DMA((len(recv),)),
            pltpu.SemaphoreType.DMA((2,)),
        ],
        compiler_params=pltpu.CompilerParams(collective_id=1, has_side_effects=True),
    )(o_in, q_in)


def reduce_kernel(a_ref, t_ref, out_ref, tab_ref, acc, s1, r1, sx, rx, sum2, sz, rz, sy, ry, tx, tz, t2, send_sem, recv_sem):
    y, x, z, c = place()
    right, left, across = lax.rem(x + 1, NX), lax.rem(x + 3, NX), lax.rem(x + 2, NX)
    pair = at(y, x, z, 1 - c)
    others = [pair, at(1 - y, x, z, c)]
    others += [at(y, lax.rem(x + i, NX), z, c) for i in range(1, NX)]
    others += [at(y, x, lax.rem(z + i, NZ), c) for i in range(1, NZ)]
    greet(others)
    count = [0]
    sent = []

    def copy(src, dst, to, here):
        i = count[0]
        count[0] += 1
        out = pltpu.make_async_remote_copy(
            src_ref=src, dst_ref=dst, send_sem=send_sem.at[i], recv_sem=recv_sem.at[i], device_id=to, device_id_type=MESH
        )
        out.start()
        sent.append(out)
        return pltpu.make_async_remote_copy(
            src_ref=src, dst_ref=here, send_sem=send_sem.at[i], recv_sem=recv_sem.at[i], device_id=to, device_id_type=MESH
        )

    s1[...] = a_ref[:, :, :, 1 - c].astype(jnp.bfloat16)
    t_pair = copy(t_ref, t2.at[0], pair, t2.at[0])
    got1 = copy(s1, r1, pair, r1)
    t_pair.wait_recv()
    t2[1] = t_ref[...] + t2[0]
    tx[x] = t2[1]
    waits = [
        copy(t2.at[1], tx.at[x], at(y, lax.rem(x + i, NX), z, c), tx.at[lax.rem(x + NX - i, NX)])
        for i in range(1, NX)
    ]
    got1.wait_recv()
    acc[...] = a_ref[:, :, :, c] + r1[...].astype(jnp.float32)
    sx[0, 0] = acc[0, across].astype(jnp.bfloat16)
    sx[1, 0] = acc[1, across].astype(jnp.bfloat16)
    gp = copy(sx.at[0, 0], rx.at[0, 0], at(y, right, z, c), rx.at[0, 0])
    gm = copy(sx.at[1, 0], rx.at[1, 0], at(y, left, z, c), rx.at[1, 0])
    for w in waits:
        w.wait_recv()
    t2[2] = ((tx[0] + tx[1]) + tx[2]) + tx[3]
    tz[z] = t2[2]
    waits = [
        copy(t2.at[2], tz.at[z], at(y, x, lax.rem(z + i, NZ), c), tz.at[lax.rem(z + NZ - i, NZ)])
        for i in range(1, NZ)
    ]
    sx[0, 2] = acc[1, right].astype(jnp.bfloat16)
    sx[1, 2] = acc[0, left].astype(jnp.bfloat16)
    g2 = [copy(sx.at[0, 2], rx.at[0, 2], at(y, right, z, c), rx.at[0, 2])]
    g2 += [copy(sx.at[1, 2], rx.at[1, 2], at(y, left, z, c), rx.at[1, 2])]
    gp.wait_recv()
    sx[0, 1] = (acc[0, right] + rx[0, 0].astype(jnp.float32)).astype(jnp.bfloat16)
    g2 += [copy(sx.at[0, 1], rx.at[0, 1], at(y, right, z, c), rx.at[0, 1])]
    gm.wait_recv()
    sx[1, 1] = (acc[1, left] + rx[1, 0].astype(jnp.float32)).astype(jnp.bfloat16)
    g2 += [copy(sx.at[1, 1], rx.at[1, 1], at(y, left, z, c), rx.at[1, 1])]
    for w in g2:
        w.wait_recv()
    sum2[0] = acc[0, x] + rx[0, 1].astype(jnp.float32) + rx[1, 2].astype(jnp.float32)
    sum2[1] = acc[1, x] + rx[0, 2].astype(jnp.float32) + rx[1, 1].astype(jnp.float32)
    zwaits = []
    for i in range(1, NZ):
        to = lax.rem(z + i, NZ)
        sz[i, 0] = sum2[0, to].astype(jnp.bfloat16)
        sz[i, 1] = sum2[1, to].astype(jnp.bfloat16)
    for i in (1, 7, 2, 6, 3, 5, 4):
        to = lax.rem(z + i, NZ)
        zwaits.append(copy(sz.at[i], rz.at[i], at(y, x, to, c), rz.at[i]))
    for w in waits:
        w.wait_recv()
    total = tz[0]
    for i in range(1, NZ):
        total = total + tz[i]
    t2[3] = total
    ty = copy(t2.at[3], t2.at[4], at(1 - y, x, z, c), t2.at[4])
    for w in zwaits:
        w.wait_recv()
    own = sum2[y, z]
    far = sum2[1 - y, z]
    for i in range(1, NZ):
        own = own + rz[i, y].astype(jnp.float32)
        far = far + rz[i, 1 - y].astype(jnp.float32)
    sy[...] = far.astype(jnp.bfloat16)
    gy = copy(sy, ry, at(1 - y, x, z, c), ry)
    ty.wait_recv()
    tab_ref[...] = (t2[3] + t2[4]) * (1.0 / 128)
    gy.wait_recv()
    out_ref[...] = (own + ry[...].astype(jnp.float32)) * (1.0 / 128)
    for s in sent:
        s.wait_send()


def reduce_grads(adapter_part, table_part):
    rows, rank = adapter_part.shape
    piece = rows // 128
    a = adapter_part.reshape(NY, NX, NZ, NC, piece, rank)
    bf, f32 = jnp.bfloat16, jnp.float32
    t_shape = (table_part.size // 128, 128)
    out, tab = pl.pallas_call(
        reduce_kernel,
        name="reduce_grads",
        out_shape=[jax.ShapeDtypeStruct((piece, rank), f32), jax.ShapeDtypeStruct(t_shape, f32)],
        in_specs=[pl.BlockSpec(memory_space=pltpu.VMEM)] * 2,
        out_specs=[pl.BlockSpec(memory_space=pltpu.VMEM)] * 2,
        scratch_shapes=[
            pltpu.VMEM((NY, NX, NZ, piece, rank), f32),
            pltpu.VMEM((NY, NX, NZ, piece, rank), bf),
            pltpu.VMEM((NY, NX, NZ, piece, rank), bf),
            pltpu.VMEM((2, 3, NZ, piece, rank), bf),
            pltpu.VMEM((2, 3, NZ, piece, rank), bf),
            pltpu.VMEM((NY, NZ, piece, rank), f32),
            pltpu.VMEM((NZ, NY, piece, rank), bf),
            pltpu.VMEM((NZ, NY, piece, rank), bf),
            pltpu.VMEM((piece, rank), bf),
            pltpu.VMEM((piece, rank), bf),
            pltpu.VMEM((NX,) + t_shape, f32),
            pltpu.VMEM((NZ,) + t_shape, f32),
            pltpu.VMEM((5,) + t_shape, f32),
            pltpu.SemaphoreType.DMA((27,)),
            pltpu.SemaphoreType.DMA((27,)),
        ],
        compiler_params=pltpu.CompilerParams(collective_id=2, has_side_effects=True),
    )(a, table_part.reshape(t_shape))
    return out, tab.reshape(table_part.shape)


def pair_blocks(frozen_out, frozen_qkv):
    c = lax.axis_index("dp") % 2
    route = [(i, i ^ 1) for i in range(lax.axis_size("dp"))]
    both = []
    for shard in (frozen_out, frozen_qkv):
        half = shard.shape[1] // 2
        low, high = shard[:, :half], shard[:, half:]
        mine = jnp.where(c == 0, low, high)
        given = lax.ppermute(jnp.where(c == 0, high, low), "dp", route)
        both.append(jnp.where(c == 0, jnp.concatenate([mine, given]), jnp.concatenate([given, mine])))
    return both


def on_device(
    block_input,
    saved_qkv,
    cotangent,
    mod_table,
    clip_condition,
    clip_frames,
    frame_tokens,
    tile_layout,
    frozen_qkv,
    frozen_out,
    adapters,
):
    tokens_here = block_input[0]
    rows, width = tokens_here.shape
    saved = saved_qkv[0]
    inner = saved.shape[1] // 3
    heads = inner // HEAD
    slots = clip_frames.shape[1]
    tiles = tile_layout.shape[1]
    adapter_rows = adapters[0]
    down_qkv = adapter_rows[:width]
    up_qkv = adapter_rows[width : width + 3 * inner]
    down_out = adapter_rows[width + 3 * inner : width + 4 * inner]
    up_out = adapter_rows[width + 4 * inner :]
    clip_ends = jnp.cumsum(clip_frames[0] * frame_tokens[0])
    position = jnp.arange(rows, dtype=jnp.int32)
    clip_of = jnp.sum((position[:, None] >= clip_ends[None, :]).astype(jnp.int32), axis=1)
    onehot_clip = (clip_of[:, None] == jnp.arange(slots, dtype=jnp.int32)[None, :]).astype(
        jnp.float32
    )
    modulation = mod_table[0].reshape(1, 3 * width) + jnp.dot(
        onehot_clip, clip_condition[0], precision=HIGH
    )
    shift_rows = modulation[:, :width]
    scale_rows = modulation[:, width : 2 * width]
    gate_rows = modulation[:, 2 * width :]
    inputs_f = tokens_here.astype(jnp.float32)
    centered = inputs_f - jnp.mean(inputs_f, axis=1, keepdims=True)
    inverse = lax.rsqrt(jnp.mean(centered * centered, axis=1, keepdims=True) + EPSILON)
    normed = centered * inverse
    modded = (normed * (1.0 + scale_rows) + shift_rows).astype(jnp.bfloat16)
    tile_onehot = (
        (position // TILE)[:, None] == jnp.arange(tiles, dtype=jnp.int32)[None, :]
    ).astype(jnp.float32)
    live_rows = jnp.dot(tile_onehot, tile_layout[0].astype(jnp.float32), precision=HIGH)
    live_pairs = jnp.dot(live_rows, tile_onehot.T, precision=HIGH) > 0.5
    allowed = live_pairs & (clip_of[:, None] == clip_of[None, :])
    queries = saved[:, :inner].reshape(rows, heads, HEAD)
    key_rows = saved[:, inner : 2 * inner].reshape(rows, heads, HEAD)
    value_rows = saved[:, 2 * inner :].reshape(rows, heads, HEAD)
    factor = HEAD ** (-0.5)
    scores = (
        jnp.einsum("qhd,khd->hqk", queries, key_rows, preferred_element_type=jnp.float32) * factor
    )
    scores = jnp.where(allowed[None], scores, -jnp.inf)
    probs = jax.nn.softmax(scores, axis=2)
    probs_b = probs.astype(jnp.bfloat16)
    attention = (
        jnp.einsum("hqk,khd->qhd", probs_b, value_rows, preferred_element_type=jnp.float32)
        .reshape(rows, inner)
        .astype(jnp.bfloat16)
    )
    out_pairs, qkv_pairs = pair_blocks(frozen_out[0], frozen_qkv[0])
    out_halves, qkv_halves = gather_weights(out_pairs, qkv_pairs)
    out_halves = out_halves.reshape(2, inner, width // 2)
    qkv_halves = qkv_halves.reshape(2, width, 3 * inner // 2)
    low_out = jnp.dot(attention, down_out, preferred_element_type=jnp.float32).astype(jnp.bfloat16)
    branch = jnp.concatenate(
        [jnp.dot(attention, half, preferred_element_type=jnp.float32) for half in out_halves], axis=1
    ) + contract_last(low_out, up_out)
    cotangent_f = cotangent[0].astype(jnp.float32)
    gated = (gate_rows * cotangent_f).astype(jnp.bfloat16)
    low_grad_out = jnp.dot(gated, up_out, preferred_element_type=jnp.float32).astype(jnp.bfloat16)
    grad_attention = (
        contract_last(gated[:, : width // 2], out_halves[0])
        + contract_last(gated[:, width // 2 :], out_halves[1])
        + contract_last(low_grad_out, down_out)
    ).astype(jnp.bfloat16)
    grad_heads = grad_attention.reshape(rows, heads, HEAD)
    grad_probs = jnp.einsum(
        "qhd,khd->hqk", grad_heads, value_rows, preferred_element_type=jnp.float32
    )
    delta = jnp.sum(probs * grad_probs, axis=2, keepdims=True)
    grad_scores = (probs * (grad_probs - delta) * factor).astype(jnp.bfloat16)
    grad_query = jnp.einsum(
        "hqk,khd->qhd", grad_scores, key_rows, preferred_element_type=jnp.float32
    ).reshape(rows, inner)
    grad_key = jnp.einsum(
        "hqk,qhd->khd", grad_scores, queries, preferred_element_type=jnp.float32
    ).reshape(rows, inner)
    grad_value = jnp.einsum(
        "hqk,qhd->khd", probs_b, grad_heads, preferred_element_type=jnp.float32
    ).reshape(rows, inner)
    grad_qkv = jnp.concatenate([grad_query, grad_key, grad_value], axis=1).astype(jnp.bfloat16)
    low_in = jnp.dot(modded, down_qkv, preferred_element_type=jnp.float32).astype(jnp.bfloat16)
    low_grad_in = jnp.dot(grad_qkv, up_qkv, preferred_element_type=jnp.float32).astype(jnp.bfloat16)
    grad_modded = (
        contract_last(grad_qkv[:, : 3 * inner // 2], qkv_halves[0])
        + contract_last(grad_qkv[:, 3 * inner // 2 :], qkv_halves[1])
        + contract_last(low_grad_in, down_qkv)
    )
    grad_normed = grad_modded * (1.0 + scale_rows)
    grad_input = cotangent_f + inverse * (
        grad_normed
        - jnp.mean(grad_normed, axis=1, keepdims=True)
        - normed * jnp.mean(grad_normed * normed, axis=1, keepdims=True)
    )
    grad_input = grad_input.astype(jnp.bfloat16)
    table_part = jnp.stack(
        [
            jnp.sum(grad_modded, axis=0),
            jnp.sum(grad_modded * normed, axis=0),
            jnp.sum(cotangent_f * branch, axis=0),
        ]
    )
    adapter_part = jnp.concatenate(
        [
            contract_first(modded, low_grad_in),
            contract_first(grad_qkv, low_in),
            contract_first(attention, low_grad_out),
            contract_first(gated, low_out),
        ],
        axis=0,
    )
    passed_back = passed_along(grad_input, "pipe", -1)
    adapter_mean, table_mean = reduce_grads(adapter_part, table_part)
    return (passed_back[None], table_mean[None], adapter_mean[None])


def solution(mesh):
    placed = (
        P("pipe", "dp", None),
        P("pipe", "dp", None),
        P("pipe", "dp", None),
        P("pipe", None, None),
        P("pipe", "dp", None),
        P("pipe", "dp"),
        P("pipe", "dp"),
        P("pipe", "dp", None),
        P("pipe", "dp", None),
        P("pipe", "dp", None),
        P("pipe", None, None),
    )
    return jax.shard_map(
        on_device,
        mesh=mesh,
        in_specs=placed,
        out_specs=(P("pipe", "dp", None), P("pipe", None, None), P("pipe", "dp", None)),
        check_vma=False,
    )
```
